768 devices in a mesh: ctx: 32 (over y, z_lo), dp: 24 (over x, z_hi, core).
Axes of the slice: x: 4, y: 8, z: 12 (z_hi: 3, z_lo: 4; z = z_hi * 4 + z_lo), core: 2. Of those that a mesh axis runs over, the one named last changes fastest.
Arguments:
- queries: bfloat16 [24, 4096, 2048], P('dp', 'ctx'), may hold values from -110 to 110
- keys: bfloat16 [24, 4096, 512], P('dp', 'ctx'), may hold values from -4 to 4
- values: bfloat16 [24, 4096, 512], P('dp', 'ctx'), may hold values from -4 to 4
- grad_out: bfloat16 [24, 4096, 2048], P('dp', 'ctx'), may hold values from -12 to 12
- sinks: float32 [16], replicated, may hold values from 0 to 6
- doc_ids: int32 [24, 32], P('dp'), may hold values from 0 to 7, never falling along the last dimension, each value on 1 to 16 neighbouring positions
Outputs:
- grad_queries: bfloat16 [24, 4096, 2048], P('dp', 'ctx')
- grad_keys: bfloat16 [24, 4096, 512], P('dp', 'ctx')
- grad_values: bfloat16 [24, 4096, 512], P('dp', 'ctx')
- grad_sinks: float32 [16], replicated
The draws below stay inside these ranges and needn't reach their ends.
All inputs are finite; a program needn't handle non-finite values.
Results may differ from the reference program's by a relative error of at most 0.017.
Values may be sent and summed in bfloat16 or wider, within the bound.
A program may use at most 32 MiB of HBM per device.

```python
import math
import jax
import jax.numpy as jnp
import numpy as np
from jax import lax

H = 16
KVH = 4
HD = 128
BLOCK = 128
WINDOW = 512
SEQLEN = 4096
SEQS = 24
NBLK = 32


def draw_pair(key):
    key_query = jax.random.fold_in(key, 11)
    key_key = jax.random.fold_in(key, 12)
    keys_raw = jnp.clip(jax.random.normal(key_key, (SEQS, SEQLEN, KVH, HD), jnp.float32), -4.0, 4.0)
    query_raw = jnp.clip(jax.random.normal(key_query, (SEQS, SEQLEN, H, HD), jnp.float32), -4.0, 4.0)
    return (query_raw.reshape(SEQS, SEQLEN, H * HD), keys_raw.reshape(SEQS, SEQLEN, KVH * HD))


def draw_queries(key, part):
    return draw_pair(key)[0].astype(jnp.bfloat16)


def draw_keys(key, part):
    return draw_pair(key)[1].astype(jnp.bfloat16)


def draw_grad_out(key, part):
    positions = jnp.arange(SEQLEN, dtype=jnp.float32) / (SEQLEN - 1)
    sequence_rank = jnp.arange(SEQS, dtype=jnp.float32) / max(SEQS - 1, 1)
    ramp = (1.0 + 2.0 * positions)[None, :, None] * (1.0 + 2.0 * sequence_rank)[:, None, None] / 3.0
    base = jnp.clip(jax.random.normal(key, (SEQS, SEQLEN, H * HD), jnp.float32), -4.0, 4.0)
    return (base * ramp).astype(jnp.bfloat16)


def block_scale(key, shape, shards, smallest, high):
    def one(position, shards_of):
        steps = jax.random.uniform(jax.random.fold_in(jax.random.fold_in(key, 6), position), (shards_of,), jnp.float32, smallest / len(shards), high / len(shards))
        return jnp.repeat(jnp.exp(steps), shape[position] // shards_of).reshape((-1,) + (1,) * (len(shape) - position - 1))

    factor_of = one(*shards[0])
    for cut in shards[1:]:
        factor_of = factor_of * one(*cut)
    return factor_of


def profile(amount, total, limit, skew):
    portions = [(1 << 20) // math.isqrt(standing ** skew) + 1 for standing in range(2, amount + 1)]
    rest, counts = total - limit - (amount - 1), [1] * (amount - 1)
    while rest > 0:
        candidates = [i for i in range(amount - 1) if counts[i] < limit]
        mass, remaining = sum([portions[i] for i in candidates]), rest
        for i in candidates:
            addition = min(limit - counts[i], max(1, remaining * portions[i] // mass), rest)
            counts[i] = counts[i] + addition
            rest = rest - addition
    return np.array([limit] + counts)


def ragged_sizes(key, count, total, most, lean):
    if count == 2:
        one = jax.random.randint(key, (), max(1, total - most), min(most, total - 1) + 1)
        return jnp.stack([one, total - one])
    sizes = jnp.asarray(profile(count, total, most, lean), jnp.int32)
    pairs = (count - 1) // 2
    source_of, receiver = sizes[1:1 + 2 * pairs:2], sizes[2:2 + 2 * pairs:2]
    room = jnp.minimum(source_of - 1, most - receiver)
    passed = jax.random.randint(jax.random.fold_in(key, 1), (pairs,), 0, 1 << 20) % (room + 1)
    sizes = sizes.at[1:1 + 2 * pairs:2].set(source_of - passed).at[2:2 + 2 * pairs:2].set(receiver + passed)
    return sizes[jax.random.permutation(jax.random.fold_in(key, 2), count)]


def scatter_about(stream_key, dims, scale, bound, split=(), kind=jnp.bfloat16):
    result = scale * jax.random.normal(stream_key, dims, jnp.float32)
    if split:
        result = result * block_scale(stream_key, dims, split, -0.22, 0.18)
    return jnp.clip(result, -bound, bound).astype(kind)


def setup_inputs(seed: int = 0) -> dict:
    arg_keys = jax.random.split(jax.random.key(seed), 7)
    return {
        "queries": draw_queries(jax.random.fold_in(arg_keys[6], 71), 0),
        "keys": draw_keys(jax.random.fold_in(arg_keys[6], 71), 0),
        "values": scatter_about(arg_keys[2], (SEQS, SEQLEN, KVH * HD), 1.0, 4.0, ((0, 24), (1, 32))),
        "grad_out": draw_grad_out(jax.random.fold_in(arg_keys[6], 71), 0),
        "sinks": jnp.clip(jax.random.uniform(arg_keys[4], (H,), jnp.float32, 0.0, 6.0), 0.0, 6.0),
        "doc_ids": jax.vmap(lambda own: jnp.searchsorted(jnp.cumsum(ragged_sizes(own, NBLK // 4, NBLK, NBLK // 2, 2)), jnp.arange(NBLK), side="right"))(jax.random.split(arg_keys[5], SEQS)).reshape((SEQS, NBLK)).astype(jnp.int32),
    }


def one_sequence(queries, keys, values, grad_out, doc_row, sinks):
    length = queries.shape[0]
    group_size = H // KVH
    score_scale = HD ** -0.5
    key_count = WINDOW + BLOCK
    pad_keys = jnp.concatenate([jnp.zeros((WINDOW, KVH * HD), jnp.bfloat16), keys], axis=0)
    pad_values = jnp.concatenate([jnp.zeros((WINDOW, KVH * HD), jnp.bfloat16), values], axis=0)
    doc_pos = jnp.concatenate([jnp.full((WINDOW,), -1, jnp.int32), jnp.repeat(doc_row, BLOCK).astype(jnp.int32)])
    sink_grid = sinks.reshape(KVH, group_size)[:, :, None]

    def block_step(carried, start_row):
        key_grad, value_grad, sink_grad = carried
        q_block = lax.dynamic_slice_in_dim(queries, start_row, BLOCK, 0).reshape(BLOCK, KVH, group_size, HD).astype(jnp.float32)
        g_block = lax.dynamic_slice_in_dim(grad_out, start_row, BLOCK, 0).reshape(BLOCK, KVH, group_size, HD).astype(jnp.float32)
        k_block = lax.dynamic_slice_in_dim(pad_keys, start_row, key_count, 0).reshape(key_count, KVH, HD).astype(jnp.float32)
        v_block = lax.dynamic_slice_in_dim(pad_values, start_row, key_count, 0).reshape(key_count, KVH, HD).astype(jnp.float32)
        query_docs = lax.dynamic_slice_in_dim(doc_pos, start_row + WINDOW, BLOCK, 0)
        key_docs = lax.dynamic_slice_in_dim(doc_pos, start_row, key_count, 0)
        offsets = WINDOW + jnp.arange(BLOCK, dtype=jnp.int32)[:, None] - jnp.arange(key_count, dtype=jnp.int32)[None, :]
        allowed = (query_docs[:, None] == key_docs[None, :]) & (offsets >= 0) & (offsets < WINDOW)
        scores = jnp.einsum('tghd,kgd->ghtk', q_block, k_block) * score_scale
        masked = jnp.where(allowed[None, None], scores, -jnp.inf)
        top_score = jnp.maximum(jnp.max(masked, axis=-1), sink_grid)
        raised = jnp.exp(masked - top_score[..., None])
        sink_weight = jnp.exp(sink_grid - top_score)
        summed = sink_weight + jnp.sum(raised, axis=-1)
        probs = lax.optimization_barrier((raised / summed[..., None]).astype(jnp.bfloat16)).astype(jnp.float32)
        attended = jnp.einsum('ghtk,kgd->tghd', probs, v_block)
        delta = jnp.transpose(jnp.sum(g_block * attended, axis=-1), (1, 2, 0))
        sink_grad = sink_grad - jnp.sum(sink_weight / summed * delta, axis=-1).reshape(H)
        grad_probs = jnp.einsum('tghd,kgd->ghtk', g_block, v_block)
        grad_scores = lax.optimization_barrier((probs * (grad_probs - delta[..., None])).astype(jnp.bfloat16)).astype(jnp.float32)
        query_grad = (jnp.einsum('ghtk,kgd->tghd', grad_scores, k_block) * score_scale).astype(jnp.bfloat16).reshape(BLOCK, H * HD)
        key_part = jnp.einsum('ghtk,tghd->kgd', grad_scores, q_block) * score_scale
        value_part = jnp.einsum('ghtk,tghd->kgd', probs, g_block)
        key_grad = lax.dynamic_update_slice_in_dim(key_grad, lax.dynamic_slice_in_dim(key_grad, start_row, key_count, 0) + key_part.reshape(key_count, KVH * HD), start_row, 0)
        value_grad = lax.dynamic_update_slice_in_dim(value_grad, lax.dynamic_slice_in_dim(value_grad, start_row, key_count, 0) + value_part.reshape(key_count, KVH * HD), start_row, 0)
        return (key_grad, value_grad, sink_grad), query_grad

    starts = jnp.arange(0, length, BLOCK, dtype=jnp.int32)
    initial = (jnp.zeros((length + WINDOW, KVH * HD), jnp.float32), jnp.zeros((length + WINDOW, KVH * HD), jnp.float32), jnp.zeros((H,), jnp.float32))
    final, query_blocks = lax.scan(block_step, initial, starts)
    key_grad, value_grad, sink_grad = final
    return query_blocks.reshape(length, H * HD), key_grad[WINDOW:].astype(jnp.bfloat16), value_grad[WINDOW:].astype(jnp.bfloat16), sink_grad


def reference(queries, keys, values, grad_out, sinks, doc_ids):
    def per_sequence(items):
        return one_sequence(items[0], items[1], items[2], items[3], items[4], sinks)

    grad_q, grad_k, grad_v, sink_parts = lax.map(per_sequence, (queries, keys, values, grad_out, doc_ids))
    return grad_q, grad_k, grad_v, jnp.sum(sink_parts, axis=0)
```

```python
import functools

import jax
import jax.numpy as jnp
from jax import lax
from jax.experimental import pallas as pl
from jax.experimental.pallas import tpu as pltpu
from jax.sharding import PartitionSpec as P

MESH = pl.DeviceIdType.MESH
ROWS = 128
HEAD = 128
GROUP = 4
ROW_CHIPS = 4
SLOTS = 5
NEG = -1e30
LOG2E = 1.4426950408889634
PRE = 2


def dp_factors(count):
    if count == 24:
        return (("core", 2, 1), ("x", 4, 6), ("zh", 3, 2))
    return (("core", count, 1),)


def kernel(
    layout,
    q_hbm,
    k_hbm,
    v_hbm,
    g_hbm,
    sink_ref,
    doc_ref,
    dq_hbm,
    dk_ref,
    dv_ref,
    ds_ref,
    q_buf,
    g_buf,
    win,
    part,
    out_buf,
    back,
    dq_buf,
    *rest,
):
    chunks, ctx_count, stages = layout
    stage_bufs = rest[: len(stages)]
    stage_send = rest[len(stages) : 2 * len(stages)]
    stage_recv = rest[2 * len(stages) : 3 * len(stages)]
    load_sem, kv_sem, dq_sem, f_send, f_recv, b_send, b_recv = rest[3 * len(stages) :]
    y_count = ctx_count // ROW_CHIPS
    ctx = lax.axis_index("ctx")
    dp = lax.axis_index("dp")
    zl = ctx % ROW_CHIPS
    y = ctx // ROW_CHIPS

    def load_kv(c, which):
        source = k_hbm if which == 0 else v_hbm
        return pltpu.make_async_copy(
            source.at[0, :, pl.ds(c * HEAD, HEAD)], win.at[c, 0, which], kv_sem.at[c, which]
        )

    def load_rows(c, which):
        source, target = (q_hbm, q_buf) if which == 0 else (g_hbm, g_buf)
        return pltpu.make_async_copy(
            source.at[0, :, pl.ds(pl.multiple_of(c * GROUP * HEAD, GROUP * HEAD), GROUP * HEAD)],
            target.at[c],
            load_sem.at[c, which],
        )

    def store_dq(c):
        return pltpu.make_async_copy(
            dq_buf.at[c],
            dq_hbm.at[0, :, pl.ds(pl.multiple_of(c * GROUP * HEAD, GROUP * HEAD), GROUP * HEAD)],
            dq_sem.at[c],
        )

    def stage_info(s):
        axis, size, stride = stages[s]
        index = ctx if axis == "ctx" else dp
        return axis, size, stride, (index // stride) % size, index

    def partner(s, step):
        axis, size, stride, mine, index = stage_info(s)
        other = (mine + step) % size
        return other, {axis: index + (other - mine) * stride}

    for c in range(chunks):
        load_kv(c, 0).start()
        load_kv(c, 1).start()
    for c in range(chunks):
        load_rows(c, 0).start()
        load_rows(c, 1).start()

    barrier = pltpu.get_barrier_semaphore()
    total_partners = 0
    for s in range(len(stages)):
        for step in range(1, stages[s][1]):
            _, device = partner(s, step)
            pl.semaphore_signal(barrier, inc=1, device_id=device, device_id_type=MESH)
            total_partners += 1

    @pl.when(y == 0)
    def _():
        for d in range(1, SLOTS):

            @pl.when(zl < d)
            def _():
                win[:, d] = jnp.zeros((chunks, 2, ROWS, HEAD), jnp.bfloat16)

    for c in range(chunks):
        load_kv(c, 0).wait()
        load_kv(c, 1).wait()
    pl.semaphore_wait(barrier, total_partners)

    def forward(c, source, target, sem, step):
        return pltpu.make_async_remote_copy(
            src_ref=win.at[c, source],
            dst_ref=win.at[c, target],
            send_sem=f_send.at[c, sem],
            recv_sem=f_recv.at[c, target],
            device_id={"ctx": ctx + step},
            device_id_type=MESH,
        )

    def backward(c, source, target, step):
        return pltpu.make_async_remote_copy(
            src_ref=out_buf.at[c, source - 1],
            dst_ref=back.at[c, target],
            send_sem=b_send.at[c, source],
            recv_sem=b_recv.at[c, target],
            device_id={"ctx": ctx + step},
            device_id_type=MESH,
        )

    def send_own(c):
        @pl.when(zl < ROW_CHIPS - 1)
        def _():
            forward(c, 0, 1, 0, 1).start()

        @pl.when(y < y_count - 1)
        def _():
            forward(c, 0, 4, 5, ROW_CHIPS).start()

    def relay(c, d):
        @pl.when((zl >= d) | (y > 0))
        def _():
            forward(c, d, d, d, 0).wait_recv()

        if d < ROW_CHIPS:

            @pl.when((zl >= d) & (zl < ROW_CHIPS - 1))
            def _():
                forward(c, d, d + 1, d, 1).start()

        @pl.when((zl < d) & (zl > 0) & (y > 0))
        def _():
            forward(c, d, d - 1, d, -1).start()

    own_doc = doc_ref[0, ctx]
    penalties = []
    for d in range(SLOTS):
        same = (doc_ref[0, (ctx - d + ctx_count) % ctx_count] == own_doc) & (ctx >= d)
        penalties.append(jnp.where(same, 0.0, NEG))
    scale = HEAD ** (-0.5)

    def compute(c):
        load_rows(c, 0).wait()
        load_rows(c, 1).wait()
        q_rows = q_buf[c]
        g_rows = g_buf[c]
        split = lambda a: jnp.concatenate(
            [a[:, h * HEAD : (h + 1) * HEAD] for h in range(GROUP)], axis=0
        )
        q = split(q_rows)
        g = split(g_rows)
        k = win[c, :, 0].reshape(SLOTS * ROWS, HEAD)
        v = win[c, :, 1].reshape(SLOTS * ROWS, HEAD)
        key_pos = lax.broadcasted_iota(jnp.int32, (ROWS, ROWS), 0)
        query_pos = lax.broadcasted_iota(jnp.int32, (ROWS, ROWS), 1)
        near = jnp.where(key_pos <= query_pos, 0.0, NEG)
        far = jnp.where(key_pos > query_pos, penalties[4], NEG)
        biases = [near, penalties[1], penalties[2], penalties[3], far]
        dims = (((1,), (1,)), ((), ()))
        s_all = lax.dot_general(k, q, dims, preferred_element_type=jnp.float32)
        dp_all = lax.dot_general(v, g, dims, preferred_element_type=jnp.float32)
        p_cols, ds_cols = [], []
        for h in range(GROUP):
            cols = slice(h * ROWS, (h + 1) * ROWS)
            sink = sink_ref[c * GROUP + h] * LOG2E
            x = [
                s_all[d * ROWS : (d + 1) * ROWS, cols] * (scale * LOG2E) + biases[d]
                for d in range(SLOTS)
            ]
            joined = functools.reduce(jnp.maximum, x)
            top = jnp.maximum(jnp.max(joined, axis=0, keepdims=True), sink)
            e = [jnp.exp2(a - top) for a in x]
            sink_weight = jnp.exp2(sink - top)
            summed = sink_weight + jnp.sum(
                functools.reduce(jnp.add, e), axis=0, keepdims=True
            )
            inverse = 1.0 / summed
            p = [(a * inverse).astype(jnp.bfloat16) for a in e]
            wide = [a.astype(jnp.float32) for a in p]
            dp_h = [dp_all[d * ROWS : (d + 1) * ROWS, cols] for d in range(SLOTS)]
            delta = jnp.sum(
                functools.reduce(jnp.add, [a * b for a, b in zip(wide, dp_h)]),
                axis=0,
                keepdims=True,
            )
            ds = [(a * (b - delta)).astype(jnp.bfloat16) for a, b in zip(wide, dp_h)]
            p_cols.append(jnp.concatenate(p, axis=0))
            ds_cols.append(jnp.concatenate(ds, axis=0))
            stage_bufs[0][stage_info(0)[3], pl.ds(c * GROUP + h, 1), :] = -(
                sink_weight * inverse * delta
            )
        p_all = jnp.concatenate(p_cols, axis=1)
        ds_all = jnp.concatenate(ds_cols, axis=1)
        dv = jnp.dot(p_all, g, preferred_element_type=jnp.float32)
        dk = jnp.dot(ds_all, q, preferred_element_type=jnp.float32) * scale
        for d in range(SLOTS):
            part[c, d, 0] = dk[d * ROWS : (d + 1) * ROWS]
            part[c, d, 1] = dv[d * ROWS : (d + 1) * ROWS]

        def query_grads():
            dq_t = jnp.dot(k.T, ds_all, preferred_element_type=jnp.float32) * scale
            for h in range(GROUP):
                dq_buf[c, :, h * HEAD : (h + 1) * HEAD] = jnp.transpose(
                    dq_t[:, h * ROWS : (h + 1) * ROWS]
                ).astype(jnp.bfloat16)
            store_dq(c).start()

        return query_grads

    def pass_back(c, d, received, target, step):
        value = part[c, d]
        if received:
            backward(c, d, d, step).wait_recv()
            value = value + back[c, d].astype(jnp.float32)
        out_buf[c, d - 1] = value.astype(jnp.bfloat16)
        backward(c, d, target, step).start()

    def wave(w, c):
        @pl.when(zl == ROW_CHIPS - 1 - w)
        def _():
            for d in range(ROW_CHIPS - 1 - w, 0, -1):
                pass_back(c, d, w > 0, d - 1, -1)

        @pl.when((zl == w) & (y > 0))
        def _():
            for d in range(w + 1, SLOTS):
                if d < ROW_CHIPS:
                    pass_back(c, d, w > 0, d + 1, 1)
                else:
                    pass_back(c, d, w > 0, 5, -ROW_CHIPS)

    def stage_start(s):
        _, size, _, mine, _ = stage_info(s)
        for step in range(1, size):
            _, device = partner(s, step)
            pltpu.make_async_remote_copy(
                src_ref=stage_bufs[s].at[mine],
                dst_ref=stage_bufs[s].at[mine],
                send_sem=stage_send[s].at[step],
                recv_sem=stage_recv[s].at[mine],
                device_id=device,
                device_id_type=MESH,
            ).start()

    def stage_copy(s, step):
        _, size, _, mine, _ = stage_info(s)
        other, device = partner(s, step)
        return pltpu.make_async_remote_copy(
            src_ref=stage_bufs[s].at[mine],
            dst_ref=stage_bufs[s].at[other],
            send_sem=stage_send[s].at[step],
            recv_sem=stage_recv[s].at[other],
            device_id=device,
            device_id_type=MESH,
        )

    def stage_finish(s):
        size = stages[s][1]
        for step in range(1, size):
            stage_copy(s, step).wait_recv()
        total = stage_bufs[s][0]
        for i in range(1, size):
            total = total + stage_bufs[s][i]
        if s + 1 < len(stages):
            stage_bufs[s + 1][stage_info(s + 1)[3]] = total
            stage_start(s + 1)
        else:
            ds_ref[...] = total

    for c in range(min(PRE, chunks)):
        send_own(c)

    def step_body(t, carry):
        @pl.when(t + PRE < chunks)
        def _():
            send_own(t + PRE)

        for d in (4, 1, 3, 2):
            relay(t, d)
        query_grads = compute(t)
        wave(0, t)
        query_grads()
        for w in range(1, ROW_CHIPS):

            @pl.when(t >= w)
            def _():
                wave(w, t - w)

        return carry

    lax.fori_loop(0, chunks, step_body, 0)
    stage_start(0)
    for t in range(chunks, chunks + ROW_CHIPS - 1):
        for w in range(1, ROW_CHIPS):
            if 0 <= t - w < chunks:
                wave(w, t - w)
        if t - chunks < len(stages):
            stage_finish(t - chunks)
    for s in range(ROW_CHIPS - 1, len(stages) - 1):
        stage_finish(s)

    for c in range(chunks):

        @pl.when(zl < ROW_CHIPS - 1)
        def _():
            backward(c, 1, 0, 1).wait_recv()
            part[c, 0] += back[c, 0].astype(jnp.float32)

        @pl.when(y < y_count - 1)
        def _():
            backward(c, 1, 5, ROW_CHIPS).wait_recv()
            part[c, 0] += back[c, 5].astype(jnp.float32)

        dk_ref[0, :, c * HEAD : (c + 1) * HEAD] = part[c, 0, 0].astype(jnp.bfloat16)
        dv_ref[0, :, c * HEAD : (c + 1) * HEAD] = part[c, 0, 1].astype(jnp.bfloat16)

    if len(stages) > ROW_CHIPS - 1:
        stage_finish(len(stages) - 1)
    for c in range(chunks):
        store_dq(c).wait()

        @pl.when(zl < ROW_CHIPS - 1)
        def _():
            forward(c, 0, 1, 0, 1).wait_send()

        @pl.when(y < y_count - 1)
        def _():
            forward(c, 0, 4, 5, ROW_CHIPS).wait_send()

        for d in range(1, SLOTS):
            goes_right = (zl >= d) & (zl < ROW_CHIPS - 1)
            goes_left = (zl < d) & (zl > 0) & (y > 0)

            @pl.when(goes_right | goes_left)
            def _():
                forward(c, d, d, d, 1).wait_send()

            @pl.when((zl >= d) | (y > 0))
            def _():
                backward(c, d, d, 1).wait_send()

    for s in range(len(stages)):
        for step in range(1, stages[s][1]):
            stage_copy(s, step).wait_send()


def local(layout, queries, keys, values, grad_out, sinks, doc_ids):
    chunks, ctx_count, stages = layout
    rows, width = queries.shape[1:]
    heads = sinks.shape[0]
    bf16, f32 = jnp.bfloat16, jnp.float32
    anywhere = pl.BlockSpec(memory_space=pl.ANY)
    scalars = pl.BlockSpec(memory_space=pltpu.SMEM)
    vmem = pl.BlockSpec(memory_space=pltpu.VMEM)
    dma = pltpu.SemaphoreType.DMA
    grad_q, grad_k, grad_v, grad_s = pl.pallas_call(
        functools.partial(kernel, layout),
        out_shape=(
            jax.ShapeDtypeStruct(queries.shape, bf16),
            jax.ShapeDtypeStruct(keys.shape, bf16),
            jax.ShapeDtypeStruct(values.shape, bf16),
            jax.ShapeDtypeStruct((heads, ROWS), f32),
        ),
        in_specs=[anywhere] * 4 + [scalars] * 2,
        out_specs=(anywhere, vmem, vmem, vmem),
        scratch_shapes=[
            pltpu.VMEM((chunks, rows, GROUP * HEAD), bf16),
            pltpu.VMEM((chunks, rows, GROUP * HEAD), bf16),
            pltpu.VMEM((chunks, SLOTS, 2, ROWS, HEAD), bf16),
            pltpu.VMEM((chunks, SLOTS, 2, ROWS, HEAD), f32),
            pltpu.VMEM((chunks, SLOTS - 1, 2, ROWS, HEAD), bf16),
            pltpu.VMEM((chunks, SLOTS + 1, 2, ROWS, HEAD), bf16),
            pltpu.VMEM((chunks, rows, GROUP * HEAD), bf16),
        ]
        + [pltpu.VMEM((size, heads, ROWS), f32) for _, size, _ in stages]
        + [dma((size,)) for _, size, _ in stages] * 2
        + [
            dma((chunks, 2)),
            dma((chunks, 2)),
            dma((chunks,)),
            dma((chunks, 6)),
            dma((chunks, 6)),
            dma((chunks, 6)),
            dma((chunks, 6)),
        ],
        compiler_params=pltpu.CompilerParams(
            collective_id=0, has_side_effects=True, vmem_limit_bytes=67043328
        ),
    )(queries, keys, values, grad_out, sinks, doc_ids)
    return grad_q, grad_k, grad_v, jnp.sum(grad_s, axis=1)


def solution(mesh):
    ctx_count = mesh.shape["ctx"]
    stages = tuple(("dp", size, stride) for _, size, stride in dp_factors(mesh.shape["dp"]))
    stages += (("ctx", ROW_CHIPS, 1), ("ctx", ctx_count // ROW_CHIPS, ROW_CHIPS))
    layout = (4, ctx_count, stages)
    split = P("dp", "ctx", None)
    return jax.shard_map(
        functools.partial(local, layout),
        mesh=mesh,
        in_specs=(split, split, split, split, P(), P("dp", None)),
        out_specs=(split, split, split, P()),
        check_vma=False,
    )
```

```python
import functools

import jax
import jax.numpy as jnp
from jax import lax
from jax.experimental import pallas as pl
from jax.experimental.pallas import tpu as pltpu
from jax.sharding import PartitionSpec as P

MESH = pl.DeviceIdType.MESH
ROWS = 128
HEAD = 128
GROUP = 4
ROW_CHIPS = 4
SLOTS = 5
NEG = -1e30
LOG2E = 1.4426950408889634
PRE = 4
LAG = 3
DIRECT = 1
PIECES = 4


def reduction_stages(ctx_count, dp_count):
    row = ("ctx", ROW_CHIPS, 1)
    column = ("ctx", ctx_count // ROW_CHIPS, ROW_CHIPS)
    if dp_count == 24:
        core, x, z_hi = ("dp", 2, 1), ("dp", 4, 6), ("dp", 3, 2)
        return ((core, x), (z_hi, row), (column,))
    return ((("dp", dp_count, 1),), (row,), (column,))


def members(stage):
    count = 1
    for _, size, _ in stage:
        count *= size
    return count


def kernel(
    layout,
    q_hbm,
    k_hbm,
    v_hbm,
    g_hbm,
    sink_ref,
    doc_ref,
    dq_hbm,
    dk_ref,
    dv_ref,
    ds_ref,
    q_buf,
    g_buf,
    win,
    part,
    out_buf,
    back,
    dq_buf,
    sink_rows,
    *rest,
):
    chunks, ctx_count, stages = layout
    stage_bufs = rest[: len(stages)]
    stage_send = rest[len(stages) : 2 * len(stages)]
    stage_recv = rest[2 * len(stages) : 3 * len(stages)]
    load_sem, kv_sem, dq_sem, f_send, f_recv, b_send, b_recv = rest[3 * len(stages) :]
    y_count = ctx_count // ROW_CHIPS
    chained = chunks - DIRECT
    ctx = lax.axis_index("ctx")
    dp = lax.axis_index("dp")
    zl = ctx % ROW_CHIPS
    y = ctx // ROW_CHIPS

    def load_kv(c, which):
        source = k_hbm if which == 0 else v_hbm
        return pltpu.make_async_copy(
            source.at[0, :, pl.ds(c * HEAD, HEAD)], win.at[c, 0, which], kv_sem.at[c, which]
        )

    def load_rows(c, which):
        source, target = (q_hbm, q_buf) if which == 0 else (g_hbm, g_buf)
        return pltpu.make_async_copy(
            source.at[0, :, pl.ds(pl.multiple_of(c * GROUP * HEAD, GROUP * HEAD), GROUP * HEAD)],
            target.at[c],
            load_sem.at[c, which],
        )

    def store_dq(c):
        return pltpu.make_async_copy(
            dq_buf.at[c],
            dq_hbm.at[0, :, pl.ds(pl.multiple_of(c * GROUP * HEAD, GROUP * HEAD), GROUP * HEAD)],
            dq_sem.at[c],
        )

    where = {"ctx": ctx, "dp": dp}

    def place(s):
        total = 0
        for axis, size, stride in stages[s]:
            total = total * size + (where[axis] // stride) % size
        return total

    def partner(s, step):
        other = (place(s) + step) % members(stages[s])
        device, rest_of = {}, other
        for axis, size, stride in reversed(stages[s]):
            mine = (where[axis] // stride) % size
            move = (rest_of % size - mine) * stride
            device[axis] = device.get(axis, where[axis]) + move
            rest_of = rest_of // size
        return other, device

    for c in range(chunks):
        load_kv(c, 0).start()
        load_kv(c, 1).start()
    for c in range(chunks):
        load_rows(c, 0).start()
        load_rows(c, 1).start()

    barrier = pltpu.get_barrier_semaphore()
    total_partners = 0
    for s in range(len(stages)):
        for step in range(1, members(stages[s])):
            _, device = partner(s, step)
            pl.semaphore_signal(barrier, inc=1, device_id=device, device_id_type=MESH)
            total_partners += 1
    for step in (1, 2, 3, -1, -2, -3):
        near = {"ctx": (ctx + step + ctx_count) % ctx_count}
        pl.semaphore_signal(barrier, inc=1, device_id=near, device_id_type=MESH)
        total_partners += 1

    @pl.when(y == 0)
    def _():
        for d in range(1, SLOTS):

            @pl.when(zl < d)
            def _():
                win[:, d] = jnp.zeros((chunks, 2, ROWS, HEAD), jnp.bfloat16)

    for c in range(chunks):
        load_kv(c, 0).wait()
        load_kv(c, 1).wait()
    pl.semaphore_wait(barrier, total_partners)

    def forward(c, source, target, sem, step):
        return pltpu.make_async_remote_copy(
            src_ref=win.at[c, source],
            dst_ref=win.at[c, target],
            send_sem=f_send.at[c, sem],
            recv_sem=f_recv.at[c, target],
            device_id={"ctx": ctx + step},
            device_id_type=MESH,
        )

    def backward(c, source, target, step):
        return pltpu.make_async_remote_copy(
            src_ref=out_buf.at[c, source - 1],
            dst_ref=back.at[c, target],
            send_sem=b_send.at[c, source],
            recv_sem=b_recv.at[c, target],
            device_id={"ctx": ctx + step},
            device_id_type=MESH,
        )

    def send_own(c):
        @pl.when(zl < ROW_CHIPS - 1)
        def _():
            forward(c, 0, 1, 0, 1).start()

        @pl.when(y < y_count - 1)
        def _():
            forward(c, 0, 4, 5, ROW_CHIPS).start()

    def passes_on(d):
        leftward = (zl < d) & (zl > 0) & (y > 0)
        return leftward if d == 4 else ((zl >= d) & (zl < ROW_CHIPS - 1)) | leftward

    def relay(c, d):
        @pl.when(passes_on(d))
        def _():
            forward(c, d, d, d, 1).wait_recv()

        if d < ROW_CHIPS:

            @pl.when((zl >= d) & (zl < ROW_CHIPS - 1))
            def _():
                forward(c, d, d + 1, d, 1).start()

        @pl.when((zl < d) & (zl > 0) & (y > 0))
        def _():
            forward(c, d, d - 1, d, -1).start()

    def arrive(c):
        for d in (4, 1, 3, 2):

            @pl.when(((zl >= d) | (y > 0)) & jnp.logical_not(passes_on(d)))
            def _():
                forward(c, d, d, d, 1).wait_recv()

    own_doc = doc_ref[0, ctx]
    penalties = []
    for d in range(SLOTS):
        same = (doc_ref[0, (ctx - d + ctx_count) % ctx_count] == own_doc) & (ctx >= d)
        penalties.append(jnp.where(same, 0.0, NEG))
    scale = HEAD ** (-0.5)

    def compute(c):
        load_rows(c, 0).wait()
        load_rows(c, 1).wait()
        q_rows = q_buf[c]
        g_rows = g_buf[c]
        split = lambda a: jnp.concatenate(
            [a[:, h * HEAD : (h + 1) * HEAD] for h in range(GROUP)], axis=0
        )
        q = split(q_rows)
        g = split(g_rows)
        k = win[c, :, 0].reshape(SLOTS * ROWS, HEAD)
        v = win[c, :, 1].reshape(SLOTS * ROWS, HEAD)
        key_pos = lax.broadcasted_iota(jnp.int32, (ROWS, ROWS), 0)
        query_pos = lax.broadcasted_iota(jnp.int32, (ROWS, ROWS), 1)
        near = jnp.where(key_pos <= query_pos, 0.0, NEG)
        far = jnp.where(key_pos > query_pos, penalties[4], NEG)
        biases = [near, penalties[1], penalties[2], penalties[3], far]
        dims = (((1,), (1,)), ((), ()))
        s_all = lax.dot_general(k, q, dims, preferred_element_type=jnp.float32)
        dp_all = lax.dot_general(v, g, dims, preferred_element_type=jnp.float32)
        p_cols, ds_cols = [], []
        for h in range(GROUP):
            cols = slice(h * ROWS, (h + 1) * ROWS)
            sink = sink_ref[c * GROUP + h] * LOG2E
            x = [
                s_all[d * ROWS : (d + 1) * ROWS, cols] * (scale * LOG2E) + biases[d]
                for d in range(SLOTS)
            ]
            joined = functools.reduce(jnp.maximum, x)
            top = jnp.maximum(jnp.max(joined, axis=0, keepdims=True), sink)
            e = [jnp.exp2(a - top) for a in x]
            sink_weight = jnp.exp2(sink - top)
            summed = sink_weight + jnp.sum(
                functools.reduce(jnp.add, e), axis=0, keepdims=True
            )
            inverse = 1.0 / summed
            p = [(a * inverse).astype(jnp.bfloat16) for a in e]
            wide = [a.astype(jnp.float32) for a in p]
            dp_h = [dp_all[d * ROWS : (d + 1) * ROWS, cols] for d in range(SLOTS)]
            delta = jnp.sum(
                functools.reduce(jnp.add, [a * b for a, b in zip(wide, dp_h)]),
                axis=0,
                keepdims=True,
            )
            ds = [(a * (b - delta)).astype(jnp.bfloat16) for a, b in zip(wide, dp_h)]
            p_cols.append(jnp.concatenate(p, axis=0))
            ds_cols.append(jnp.concatenate(ds, axis=0))
            sink_rows[pl.ds(c * GROUP + h, 1), :] = -(sink_weight * inverse * delta)
        p_all = jnp.concatenate(p_cols, axis=1)
        ds_all = jnp.concatenate(ds_cols, axis=1)
        dv = jnp.dot(p_all, g, preferred_element_type=jnp.float32)
        dk = jnp.dot(ds_all, q, preferred_element_type=jnp.float32) * scale
        for d in range(SLOTS):
            part[c, d, 0] = dk[d * ROWS : (d + 1) * ROWS]
            part[c, d, 1] = dv[d * ROWS : (d + 1) * ROWS]

        def query_grads():
            dq_t = jnp.dot(k.T, ds_all, preferred_element_type=jnp.float32) * scale
            for h in range(GROUP):
                dq_buf[c, :, h * HEAD : (h + 1) * HEAD] = jnp.transpose(
                    dq_t[:, h * ROWS : (h + 1) * ROWS]
                ).astype(jnp.bfloat16)
            store_dq(c).start()

        return query_grads

    def pass_back(c, d, received, target, step):
        value = part[c, d]
        if received:
            backward(c, d, d, step).wait_recv()
            value = value + back[c, d].astype(jnp.float32)
        out_buf[c, d - 1] = value.astype(jnp.bfloat16)
        backward(c, d, target, step).start()

    def wave(w, c):
        @pl.when(zl == ROW_CHIPS - 1 - w)
        def _():
            for d in range(ROW_CHIPS - 1 - w, 0, -1):
                pass_back(c, d, w > 0, d - 1, -1)

        @pl.when((zl == w) & (y > 0))
        def _():
            for d in range(w + 1, SLOTS):
                if d < ROW_CHIPS:
                    pass_back(c, d, w > 0, d + 1, 1)
                else:
                    pass_back(c, d, w > 0, 5, -ROW_CHIPS)

    def direct(c):
        for d in (3, 2, 1, 4):

            @pl.when(ctx >= d)
            def _():
                out_buf[c, d - 1] = part[c, d].astype(jnp.bfloat16)
                backward(c, d, d, -d).start()

    def stage_copy(s, step, outgoing):
        mine = place(s)
        other, device = partner(s, step)
        slot = mine if outgoing else other
        return pltpu.make_async_remote_copy(
            src_ref=stage_bufs[s].at[mine],
            dst_ref=stage_bufs[s].at[slot],
            send_sem=stage_send[s].at[step],
            recv_sem=stage_recv[s].at[slot],
            device_id=device,
            device_id_type=MESH,
        )

    def stage_start(s, value):
        stage_bufs[s][place(s)] = value
        for step in range(1, members(stages[s])):
            stage_copy(s, step, True).start()

    def sinks_start():
        heads = sink_rows.shape[0]
        head = lax.broadcasted_iota(jnp.int32, (heads, ROWS), 0)
        lane = lax.broadcasted_iota(jnp.int32, (heads, ROWS), 1)
        sums = jnp.sum(sink_rows[...], axis=1, keepdims=True)
        stage_start(0, jnp.sum(jnp.where(head == lane, sums, 0.0), axis=0, keepdims=True))

    def stage_finish(s):
        size = members(stages[s])
        for step in range(1, size):
            stage_copy(s, step, False).wait_recv()
        total = stage_bufs[s][0]
        for i in range(1, size):
            total = total + stage_bufs[s][i]
        if s + 1 < len(stages):
            stage_start(s + 1, total)
        else:
            ds_ref[...] = total

    for c in range(min(PRE, chunks)):
        send_own(c)

    def relays(t):
        for c, d in ((t, 4), (t, 1), (t - 1, 3), (t - 2, 2)):
            if isinstance(t, int):
                if 0 <= c < chunks:
                    relay(c, d)
            else:

                @pl.when(c < chunks)
                def _():
                    relay(c, d)

    for t in range(LAG):
        relays(t)
        if t + PRE < chunks:
            send_own(t + PRE)

    def step_body(c, carry):
        relays(c + LAG)
        arrive(c)
        query_grads = compute(c)

        @pl.when(c == chunks - 1)
        def _():
            sinks_start()

        @pl.when(c < chained)
        def _():
            wave(0, c)

        @pl.when(c >= chained)
        def _():
            direct(c)

        query_grads()
        for w in range(1, ROW_CHIPS):

            @pl.when((c >= w) & (c - w < chained))
            def _():
                wave(w, c - w)

        return carry

    lax.fori_loop(0, chunks, step_body, 0)
    for t in range(chunks, chunks + ROW_CHIPS - 1):
        if t - chunks < len(stages):
            stage_finish(t - chunks)
        for w in range(1, ROW_CHIPS):
            if 0 <= t - w < chained:
                wave(w, t - w)
    for s in range(ROW_CHIPS - 1, len(stages) - 1):
        stage_finish(s)

    for c in range(chunks):
        if c < chained:
            sources = [(0, zl < ROW_CHIPS - 1), (5, y < y_count - 1)]
        else:
            sources = [(d, ctx + d < ctx_count) for d in range(1, SLOTS)]
        for slot, exists in sources:

            @pl.when(exists)
            def _():
                backward(c, 1, slot, 1).wait_recv()
                part[c, 0] += back[c, slot].astype(jnp.float32)

        dk_ref[0, :, c * HEAD : (c + 1) * HEAD] = part[c, 0, 0].astype(jnp.bfloat16)
        dv_ref[0, :, c * HEAD : (c + 1) * HEAD] = part[c, 0, 1].astype(jnp.bfloat16)

    if len(stages) > ROW_CHIPS - 1:
        stage_finish(len(stages) - 1)
    for c in range(chunks):
        store_dq(c).wait()

        @pl.when(zl < ROW_CHIPS - 1)
        def _():
            forward(c, 0, 1, 0, 1).wait_send()

        @pl.when(y < y_count - 1)
        def _():
            forward(c, 0, 4, 5, ROW_CHIPS).wait_send()

        for d in range(1, SLOTS):
            goes_right = (zl >= d) & (zl < ROW_CHIPS - 1)
            goes_left = (zl < d) & (zl > 0) & (y > 0)

            @pl.when(goes_right | goes_left)
            def _():
                forward(c, d, d, d, 1).wait_send()

            @pl.when((zl >= d) | (y > 0))
            def _():
                backward(c, d, d, 1).wait_send()

    for s in range(len(stages)):
        for step in range(1, members(stages[s])):
            stage_copy(s, step, True).wait_send()


def hand_over(q_in, k_in, v_in, s_ref, q_out, k_out, v_out, s_out, *rest):
    buffers, arrived, stored = rest[:3], rest[3:6], rest[6:]
    arrays = ((q_in, q_out), (k_in, k_out), (v_in, v_out))
    loads, stores = [], []
    for (source, target), buffer, full, empty in zip(arrays, buffers, arrived, stored):
        count, rows = buffer.shape[:2]
        for i in range(count):
            part = pl.ds(i * rows, rows)
            loads.append(pltpu.make_async_copy(source.at[0, part], buffer.at[i], full.at[i]))
            stores.append(pltpu.make_async_copy(buffer.at[i], target.at[0, part], empty.at[i]))
    for load in loads:
        load.start()
    s_out[...] = s_ref[0, : s_out.shape[0]]
    for load, store in zip(loads, stores):
        load.wait()
        store.start()
    for store in stores:
        store.wait()


def local(layout, queries, keys, values, grad_out, sinks, doc_ids):
    chunks, ctx_count, stages = layout
    rows, width = queries.shape[1:]
    heads = sinks.shape[0]
    bf16, f32 = jnp.bfloat16, jnp.float32
    anywhere = pl.BlockSpec(memory_space=pl.ANY)
    scalars = pl.BlockSpec(memory_space=pltpu.SMEM)
    vmem = pl.BlockSpec(memory_space=pltpu.VMEM)
    dma = pltpu.SemaphoreType.DMA
    grad_q, grad_k, grad_v, grad_s = pl.pallas_call(
        functools.partial(kernel, layout),
        out_shape=(
            jax.ShapeDtypeStruct(queries.shape, bf16),
            jax.ShapeDtypeStruct(keys.shape, bf16),
            jax.ShapeDtypeStruct(values.shape, bf16),
            jax.ShapeDtypeStruct((1, ROWS), f32),
        ),
        in_specs=[anywhere] * 4 + [scalars] * 2,
        out_specs=(anywhere, vmem, vmem, vmem),
        scratch_shapes=[
            pltpu.VMEM((chunks, rows, GROUP * HEAD), bf16),
            pltpu.VMEM((chunks, rows, GROUP * HEAD), bf16),
            pltpu.VMEM((chunks, SLOTS, 2, ROWS, HEAD), bf16),
            pltpu.VMEM((chunks, SLOTS, 2, ROWS, HEAD), f32),
            pltpu.VMEM((chunks, SLOTS - 1, 2, ROWS, HEAD), bf16),
            pltpu.VMEM((chunks, SLOTS + 1, 2, ROWS, HEAD), bf16),
            pltpu.VMEM((chunks, rows, GROUP * HEAD), bf16),
            pltpu.VMEM((heads, ROWS), f32),
        ]
        + [pltpu.VMEM((members(stage), 1, ROWS), f32) for stage in stages]
        + [dma((members(stage),)) for stage in stages] * 2
        + [
            dma((chunks, 2)),
            dma((chunks, 2)),
            dma((chunks,)),
            dma((chunks, 6)),
            dma((chunks, 6)),
            dma((chunks, 6)),
            dma((chunks, 6)),
        ],
        compiler_params=pltpu.CompilerParams(
            collective_id=0, has_side_effects=True, vmem_limit_bytes=67043328
        ),
    )(queries, keys, values, grad_out, sinks, doc_ids)
    sizes = [(PIECES, rows // PIECES, width)] + [(1, rows, keys.shape[2])] * 2
    return pl.pallas_call(
        hand_over,
        out_shape=(
            jax.ShapeDtypeStruct(queries.shape, bf16),
            jax.ShapeDtypeStruct(keys.shape, bf16),
            jax.ShapeDtypeStruct(values.shape, bf16),
            jax.ShapeDtypeStruct((heads,), f32),
        ),
        in_specs=[anywhere] * 3 + [vmem],
        out_specs=(anywhere, anywhere, anywhere, vmem),
        scratch_shapes=[pltpu.VMEM(size, bf16) for size in sizes]
        + [dma((size[0],)) for size in sizes] * 2,
        compiler_params=pltpu.CompilerParams(vmem_limit_bytes=67043328),
    )(grad_q, grad_k, grad_v, grad_s)


def solution(mesh):
    ctx_count = mesh.shape["ctx"]
    stages = reduction_stages(ctx_count, mesh.shape["dp"])
    layout = (4, ctx_count, stages)
    split = P("dp", "ctx", None)
    return jax.shard_map(
        functools.partial(local, layout),
        mesh=mesh,
        in_specs=(split, split, split, split, P(), P("dp", None)),
        out_specs=(split, split, split, P()),
        check_vma=False,
    )
```

```python
import functools

import jax
import jax.numpy as jnp
from jax import lax
from jax.experimental import pallas as pl
from jax.experimental.pallas import tpu as pltpu
from jax.sharding import PartitionSpec as P

MESH = pl.DeviceIdType.MESH
ROWS = 128
HEAD = 128
GROUP = 4
ROW_CHIPS = 4
SLOTS = 5
NEG = -1e30
LOG2E = 1.4426950408889634
PRE = 4
LAG = 3
DIRECT = 1


def reduction_stages(ctx_count, dp_count):
    row = ("ctx", ROW_CHIPS, 1)
    column = ("ctx", ctx_count // ROW_CHIPS, ROW_CHIPS)
    if dp_count == 24:
        core, x, z_hi = ("dp", 2, 1), ("dp", 4, 6), ("dp", 3, 2)
        return ((core, x), (z_hi, row), (column,))
    return ((("dp", dp_count, 1),), (row,), (column,))


def members(stage):
    count = 1
    for _, size, _ in stage:
        count *= size
    return count


def kernel(
    layout,
    q_hbm,
    k_hbm,
    v_hbm,
    g_hbm,
    sink_ref,
    doc_ref,
    dq_hbm,
    dk_ref,
    dv_ref,
    ds_ref,
    q_buf,
    g_buf,
    win,
    part,
    out_buf,
    back,
    dq_buf,
    sink_rows,
    *rest,
):
    chunks, ctx_count, stages = layout
    stage_bufs = rest[: len(stages)]
    stage_send = rest[len(stages) : 2 * len(stages)]
    stage_recv = rest[2 * len(stages) : 3 * len(stages)]
    load_sem, kv_sem, dq_sem, f_send, f_recv, b_send, b_recv = rest[3 * len(stages) :]
    y_count = ctx_count // ROW_CHIPS
    chained = chunks - DIRECT
    ctx = lax.axis_index("ctx")
    dp = lax.axis_index("dp")
    zl = ctx % ROW_CHIPS
    y = ctx // ROW_CHIPS

    def load_kv(c, which):
        source = k_hbm if which == 0 else v_hbm
        return pltpu.make_async_copy(
            source.at[0, :, pl.ds(c * HEAD, HEAD)], win.at[c, 0, which], kv_sem.at[c, which]
        )

    def load_rows(c, which):
        source, target = (q_hbm, q_buf) if which == 0 else (g_hbm, g_buf)
        return pltpu.make_async_copy(
            source.at[0, :, pl.ds(pl.multiple_of(c * GROUP * HEAD, GROUP * HEAD), GROUP * HEAD)],
            target.at[c],
            load_sem.at[c, which],
        )

    def store_dq(c):
        return pltpu.make_async_copy(
            dq_buf.at[c],
            dq_hbm.at[0, :, pl.ds(pl.multiple_of(c * GROUP * HEAD, GROUP * HEAD), GROUP * HEAD)],
            dq_sem.at[c],
        )

    where = {"ctx": ctx, "dp": dp}

    def place(s):
        total = 0
        for axis, size, stride in stages[s]:
            total = total * size + (where[axis] // stride) % size
        return total

    def partner(s, step):
        other = (place(s) + step) % members(stages[s])
        device, rest_of = {}, other
        for axis, size, stride in reversed(stages[s]):
            mine = (where[axis] // stride) % size
            move = (rest_of % size - mine) * stride
            device[axis] = device.get(axis, where[axis]) + move
            rest_of = rest_of // size
        return other, device

    for c in range(chunks):
        load_kv(c, 0).start()
        load_kv(c, 1).start()
    for c in range(chunks):
        load_rows(c, 0).start()
        load_rows(c, 1).start()

    barrier = pltpu.get_barrier_semaphore()
    total_partners = 0
    for s in range(len(stages)):
        for step in range(1, members(stages[s])):
            _, device = partner(s, step)
            pl.semaphore_signal(barrier, inc=1, device_id=device, device_id_type=MESH)
            total_partners += 1
    for step in (1, 2, 3, -1, -2, -3):
        near = {"ctx": (ctx + step + ctx_count) % ctx_count}
        pl.semaphore_signal(barrier, inc=1, device_id=near, device_id_type=MESH)
        total_partners += 1

    @pl.when(y == 0)
    def _():
        for d in range(1, SLOTS):

            @pl.when(zl < d)
            def _():
                win[:, d] = jnp.zeros((chunks, 2, ROWS, HEAD), jnp.bfloat16)

    for c in range(chunks):
        load_kv(c, 0).wait()
        load_kv(c, 1).wait()
    pl.semaphore_wait(barrier, total_partners)

    def forward(c, source, target, sem, step):
        return pltpu.make_async_remote_copy(
            src_ref=win.at[c, source],
            dst_ref=win.at[c, target],
            send_sem=f_send.at[c, sem],
            recv_sem=f_recv.at[c, target],
            device_id={"ctx": ctx + step},
            device_id_type=MESH,
        )

    def backward(c, source, target, step):
        return pltpu.make_async_remote_copy(
            src_ref=out_buf.at[c, source - 1],
            dst_ref=back.at[c, target],
            send_sem=b_send.at[c, source],
            recv_sem=b_recv.at[c, target],
            device_id={"ctx": ctx + step},
            device_id_type=MESH,
        )

    def send_own(c):
        @pl.when(zl < ROW_CHIPS - 1)
        def _():
            forward(c, 0, 1, 0, 1).start()

        @pl.when(y < y_count - 1)
        def _():
            forward(c, 0, 4, 5, ROW_CHIPS).start()

    def passes_on(d):
        leftward = (zl < d) & (zl > 0) & (y > 0)
        return leftward if d == 4 else ((zl >= d) & (zl < ROW_CHIPS - 1)) | leftward

    def relay(c, d):
        @pl.when(passes_on(d))
        def _():
            forward(c, d, d, d, 1).wait_recv()

        if d < ROW_CHIPS:

            @pl.when((zl >= d) & (zl < ROW_CHIPS - 1))
            def _():
                forward(c, d, d + 1, d, 1).start()

        @pl.when((zl < d) & (zl > 0) & (y > 0))
        def _():
            forward(c, d, d - 1, d, -1).start()

    def arrive(c):
        for d in (4, 1, 3, 2):

            @pl.when(((zl >= d) | (y > 0)) & jnp.logical_not(passes_on(d)))
            def _():
                forward(c, d, d, d, 1).wait_recv()

    own_doc = doc_ref[0, ctx]
    penalties = []
    for d in range(SLOTS):
        same = (doc_ref[0, (ctx - d + ctx_count) % ctx_count] == own_doc) & (ctx >= d)
        penalties.append(jnp.where(same, 0.0, NEG))
    scale = HEAD ** (-0.5)

    def compute(c):
        load_rows(c, 0).wait()
        load_rows(c, 1).wait()
        q_rows = q_buf[c]
        g_rows = g_buf[c]
        split = lambda a: jnp.concatenate(
            [a[:, h * HEAD : (h + 1) * HEAD] for h in range(GROUP)], axis=0
        )
        q = split(q_rows)
        g = split(g_rows)
        k = win[c, :, 0].reshape(SLOTS * ROWS, HEAD)
        v = win[c, :, 1].reshape(SLOTS * ROWS, HEAD)
        key_pos = lax.broadcasted_iota(jnp.int32, (ROWS, ROWS), 0)
        query_pos = lax.broadcasted_iota(jnp.int32, (ROWS, ROWS), 1)
        near = jnp.where(key_pos <= query_pos, 0.0, NEG)
        far = jnp.where(key_pos > query_pos, penalties[4], NEG)
        biases = [near, penalties[1], penalties[2], penalties[3], far]
        dims = (((1,), (1,)), ((), ()))
        s_all = lax.dot_general(k, q, dims, preferred_element_type=jnp.float32)
        dp_all = lax.dot_general(v, g, dims, preferred_element_type=jnp.float32)
        p_cols, ds_cols = [], []
        for h in range(GROUP):
            cols = slice(h * ROWS, (h + 1) * ROWS)
            sink = sink_ref[c * GROUP + h] * LOG2E
            x = [
                s_all[d * ROWS : (d + 1) * ROWS, cols] * (scale * LOG2E) + biases[d]
                for d in range(SLOTS)
            ]
            joined = functools.reduce(jnp.maximum, x)
            top = jnp.maximum(jnp.max(joined, axis=0, keepdims=True), sink)
            e = [jnp.exp2(a - top) for a in x]
            sink_weight = jnp.exp2(sink - top)
            summed = sink_weight + jnp.sum(
                functools.reduce(jnp.add, e), axis=0, keepdims=True
            )
            inverse = 1.0 / summed
            p = [(a * inverse).astype(jnp.bfloat16) for a in e]
            wide = [a.astype(jnp.float32) for a in p]
            dp_h = [dp_all[d * ROWS : (d + 1) * ROWS, cols] for d in range(SLOTS)]
            delta = jnp.sum(
                functools.reduce(jnp.add, [a * b for a, b in zip(wide, dp_h)]),
                axis=0,
                keepdims=True,
            )
            ds = [(a * (b - delta)).astype(jnp.bfloat16) for a, b in zip(wide, dp_h)]
            p_cols.append(jnp.concatenate(p, axis=0))
            ds_cols.append(jnp.concatenate(ds, axis=0))
            sink_rows[pl.ds(c * GROUP + h, 1), :] = -(sink_weight * inverse * delta)
        p_all = jnp.concatenate(p_cols, axis=1)
        ds_all = jnp.concatenate(ds_cols, axis=1)
        dv = jnp.dot(p_all, g, preferred_element_type=jnp.float32)
        dk = jnp.dot(ds_all, q, preferred_element_type=jnp.float32) * scale
        for d in range(SLOTS):
            part[c, d, 0] = dk[d * ROWS : (d + 1) * ROWS]
            part[c, d, 1] = dv[d * ROWS : (d + 1) * ROWS]

        def query_grads():
            dq_t = jnp.dot(k.T, ds_all, preferred_element_type=jnp.float32) * scale
            for h in range(GROUP):
                dq_buf[c, :, h * HEAD : (h + 1) * HEAD] = jnp.transpose(
                    dq_t[:, h * ROWS : (h + 1) * ROWS]
                ).astype(jnp.bfloat16)
            store_dq(c).start()

        return query_grads

    def pass_back(c, d, received, target, step):
        value = part[c, d]
        if received:
            backward(c, d, d, step).wait_recv()
            value = value + back[c, d].astype(jnp.float32)
        out_buf[c, d - 1] = value.astype(jnp.bfloat16)
        backward(c, d, target, step).start()

    def wave(w, c):
        @pl.when(zl == ROW_CHIPS - 1 - w)
        def _():
            for d in range(ROW_CHIPS - 1 - w, 0, -1):
                pass_back(c, d, w > 0, d - 1, -1)

        @pl.when((zl == w) & (y > 0))
        def _():
            for d in range(w + 1, SLOTS):
                if d < ROW_CHIPS:
                    pass_back(c, d, w > 0, d + 1, 1)
                else:
                    pass_back(c, d, w > 0, 5, -ROW_CHIPS)

    def direct(c):
        for d in (3, 2, 1, 4):

            @pl.when(ctx >= d)
            def _():
                out_buf[c, d - 1] = part[c, d].astype(jnp.bfloat16)
                backward(c, d, d, -d).start()

    def stage_copy(s, step, outgoing):
        mine = place(s)
        other, device = partner(s, step)
        slot = mine if outgoing else other
        return pltpu.make_async_remote_copy(
            src_ref=stage_bufs[s].at[mine],
            dst_ref=stage_bufs[s].at[slot],
            send_sem=stage_send[s].at[step],
            recv_sem=stage_recv[s].at[slot],
            device_id=device,
            device_id_type=MESH,
        )

    def stage_start(s, value):
        stage_bufs[s][place(s)] = value
        for step in range(1, members(stages[s])):
            stage_copy(s, step, True).start()

    def sinks_start():
        heads = sink_rows.shape[0]
        head = lax.broadcasted_iota(jnp.int32, (heads, ROWS), 0)
        lane = lax.broadcasted_iota(jnp.int32, (heads, ROWS), 1)
        sums = jnp.sum(sink_rows[...], axis=1, keepdims=True)
        stage_start(0, jnp.sum(jnp.where(head == lane, sums, 0.0), axis=0, keepdims=True))

    def stage_finish(s):
        size = members(stages[s])
        for step in range(1, size):
            stage_copy(s, step, False).wait_recv()
        total = stage_bufs[s][0]
        for i in range(1, size):
            total = total + stage_bufs[s][i]
        if s + 1 < len(stages):
            stage_start(s + 1, total)
        else:
            ds_ref[...] = total

    for c in range(min(PRE, chunks)):
        send_own(c)

    def relays(t):
        for c, d in ((t, 4), (t, 1), (t - 1, 3), (t - 2, 2)):
            if isinstance(t, int):
                if 0 <= c < chunks:
                    relay(c, d)
            else:

                @pl.when(c < chunks)
                def _():
                    relay(c, d)

    for t in range(LAG):
        relays(t)
        if t + PRE < chunks:
            send_own(t + PRE)

    def step_body(c, carry):
        relays(c + LAG)
        arrive(c)
        query_grads = compute(c)

        @pl.when(c == chunks - 1)
        def _():
            sinks_start()

        @pl.when(c < chained)
        def _():
            wave(0, c)

        @pl.when(c >= chained)
        def _():
            direct(c)

        query_grads()
        for w in range(1, ROW_CHIPS):

            @pl.when((c >= w) & (c - w < chained))
            def _():
                wave(w, c - w)

        return carry

    lax.fori_loop(0, chunks, step_body, 0)
    for t in range(chunks, chunks + ROW_CHIPS - 1):
        if t - chunks < len(stages):
            stage_finish(t - chunks)
        for w in range(1, ROW_CHIPS):
            if 0 <= t - w < chained:
                wave(w, t - w)
    for s in range(ROW_CHIPS - 1, len(stages) - 1):
        stage_finish(s)

    for c in range(chunks):
        if c < chained:
            sources = [(0, zl < ROW_CHIPS - 1), (5, y < y_count - 1)]
        else:
            sources = [(d, ctx + d < ctx_count) for d in range(1, SLOTS)]
        for slot, exists in sources:

            @pl.when(exists)
            def _():
                backward(c, 1, slot, 1).wait_recv()
                part[c, 0] += back[c, slot].astype(jnp.float32)

        dk_ref[0, :, c * HEAD : (c + 1) * HEAD] = part[c, 0, 0].astype(jnp.bfloat16)
        dv_ref[0, :, c * HEAD : (c + 1) * HEAD] = part[c, 0, 1].astype(jnp.bfloat16)

    if len(stages) > ROW_CHIPS - 1:
        stage_finish(len(stages) - 1)
    for c in range(chunks):
        store_dq(c).wait()

        @pl.when(zl < ROW_CHIPS - 1)
        def _():
            forward(c, 0, 1, 0, 1).wait_send()

        @pl.when(y < y_count - 1)
        def _():
            forward(c, 0, 4, 5, ROW_CHIPS).wait_send()

        for d in range(1, SLOTS):
            goes_right = (zl >= d) & (zl < ROW_CHIPS - 1)
            goes_left = (zl < d) & (zl > 0) & (y > 0)

            @pl.when(goes_right | goes_left)
            def _():
                forward(c, d, d, d, 1).wait_send()

            @pl.when((zl >= d) | (y > 0))
            def _():
                backward(c, d, d, 1).wait_send()

    for s in range(len(stages)):
        for step in range(1, members(stages[s])):
            stage_copy(s, step, True).wait_send()


def hand_over(q_in, k_in, v_in, s_ref, q_out, k_out, v_out, s_out, stored):
    copies = [
        pltpu.make_async_copy(source, target, stored.at[i])
        for i, (source, target) in enumerate(((q_in, q_out), (k_in, k_out), (v_in, v_out)))
    ]
    for copy in copies:
        copy.start()
    s_out[...] = s_ref[0, : s_out.shape[0]]
    for copy in copies:
        copy.wait()


def local(layout, queries, keys, values, grad_out, sinks, doc_ids):
    chunks, ctx_count, stages = layout
    rows = queries.shape[1]
    heads = sinks.shape[0]
    bf16, f32 = jnp.bfloat16, jnp.float32
    anywhere = pl.BlockSpec(memory_space=pl.ANY)
    scalars = pl.BlockSpec(memory_space=pltpu.SMEM)
    vmem = pl.BlockSpec(memory_space=pltpu.VMEM)
    dma = pltpu.SemaphoreType.DMA
    operands = [
        pltpu.with_memory_space_constraint(a, pltpu.HBM)
        for a in (queries, keys, values, grad_out, sinks, doc_ids)
    ]
    grad_q, grad_k, grad_v, grad_s = pl.pallas_call(
        functools.partial(kernel, layout),
        out_shape=(
            jax.ShapeDtypeStruct(queries.shape, bf16),
            jax.ShapeDtypeStruct(keys.shape, bf16),
            jax.ShapeDtypeStruct(values.shape, bf16),
            jax.ShapeDtypeStruct((1, ROWS), f32),
        ),
        in_specs=[anywhere] * 4 + [scalars] * 2,
        out_specs=(anywhere, vmem, vmem, vmem),
        scratch_shapes=[
            pltpu.VMEM((chunks, rows, GROUP * HEAD), bf16),
            pltpu.VMEM((chunks, rows, GROUP * HEAD), bf16),
            pltpu.VMEM((chunks, SLOTS, 2, ROWS, HEAD), bf16),
            pltpu.VMEM((chunks, SLOTS, 2, ROWS, HEAD), f32),
            pltpu.VMEM((chunks, SLOTS - 1, 2, ROWS, HEAD), bf16),
            pltpu.VMEM((chunks, SLOTS + 1, 2, ROWS, HEAD), bf16),
            pltpu.VMEM((chunks, rows, GROUP * HEAD), bf16),
            pltpu.VMEM((heads, ROWS), f32),
        ]
        + [pltpu.VMEM((members(stage), 1, ROWS), f32) for stage in stages]
        + [dma((members(stage),)) for stage in stages] * 2
        + [
            dma((chunks, 2)),
            dma((chunks, 2)),
            dma((chunks,)),
            dma((chunks, 6)),
            dma((chunks, 6)),
            dma((chunks, 6)),
            dma((chunks, 6)),
        ],
        compiler_params=pltpu.CompilerParams(
            collective_id=0, has_side_effects=True, vmem_limit_bytes=24 * 1024 * 1024
        ),
    )(*operands)
    return pl.pallas_call(
        hand_over,
        out_shape=(
            jax.ShapeDtypeStruct(queries.shape, bf16),
            jax.ShapeDtypeStruct(keys.shape, bf16),
            jax.ShapeDtypeStruct(values.shape, bf16),
            jax.ShapeDtypeStruct((heads,), f32),
        ),
        in_specs=[anywhere] * 3 + [vmem],
        out_specs=(anywhere, anywhere, anywhere, vmem),
        scratch_shapes=[dma((3,))],
        compiler_params=pltpu.CompilerParams(vmem_limit_bytes=4 * 1024 * 1024),
    )(grad_q, grad_k, grad_v, grad_s)


def solution(mesh):
    ctx_count = mesh.shape["ctx"]
    stages = reduction_stages(ctx_count, mesh.shape["dp"])
    layout = (4, ctx_count, stages)
    split = P("dp", "ctx", None)
    return jax.shard_map(
        functools.partial(local, layout),
        mesh=mesh,
        in_specs=(split, split, split, split, P(), P("dp", None)),
        out_specs=(split, split, split, P()),
        check_vma=False,
    )
```
